32 devices in a mesh: groups: 1, rows: 32 (over z, y, x, core).
Axes of the slice: x: 2, y: 2, z: 4, core: 2. Of those that a mesh axis runs over, the one named last changes fastest.
Arguments:
- tokens: bfloat16 [384, 8192], P(('groups', 'rows')), may hold values from -6 to 6
- gate_weight: bfloat16 [8192, 14336], P('rows'), may hold values from -0.0625 to 0.0625
- up_weight: bfloat16 [8192, 14336], P('rows'), may hold values from -0.0625 to 0.0625
- skew_params: float32 [2, 2, 128, 64, 64], P(None, None, 'rows'), may hold values from -0.3125 to 0.3125
- section_bits: int32 [2, 13], replicated, may hold values from 0 to 12, each once within a row
- upstream: bfloat16 [384, 14336], P('groups', 'rows'), may hold values from -0.3125 to 0.3125
Outputs:
- activation: bfloat16 [384, 14336], P('groups', 'rows')
- skew_grad: float32 [2, 2, 128, 64, 64], P('groups', None, 'rows')
The draws below stay inside these ranges and needn't reach their ends.
Inputs may be any that keep to these rules, and one draw needn't show every extreme that they name: Each row of section_bits names every one of the 13 bit positions once.
All inputs are finite; a program needn't handle non-finite values.
Results may differ from the reference program's by a relative error of at most 0.0093.
Values may be sent and summed in bfloat16 or wider, within the bound.
A program may use at most 192 MiB of HBM per device.

```python
import jax
import jax.numpy as jnp
from jax import lax

D = 8192
FF = 14336
LOG_D = 13
BLOCK = 64
SECTIONS = 2
MATS = 2
TOKENS = 384
NB = 128


def block_levels(key, shape, shards, least, largest):
    factor_of = 1.0
    for position, parts in shards:
        draws = jax.random.uniform(jax.random.fold_in(jax.random.fold_in(key, 6), position), (parts,), jnp.float32, least / len(shards), largest / len(shards))
        factor_of = factor_of * jnp.repeat(jnp.exp(draws), shape[position] // parts).reshape((-1,) + (1,) * (len(shape) - 1 - position))
    return factor_of


def noise(rng, shape, width, most, split=(), held_as=jnp.bfloat16):
    level = block_levels(rng, shape, split, -0.22, 0.18) if split else 1.0
    drawn = jax.random.normal(rng, shape, jnp.float32) * width * level
    return jnp.minimum(jnp.maximum(drawn, -most), most).astype(held_as)


def setup_inputs(seed: int = 0, part: int = 0) -> dict:
    key_list = jax.random.split(jax.random.key(seed), 7)
    part_splits = jax.random.split(jax.random.fold_in(key_list[6], part), 7)
    tokens = noise(part_splits[0], (TOKENS, D), 1.0, 6.0, ((0, 32),))
    gate_weight = noise(key_list[1], (D, FF), D ** -0.5, 0.0625, ((0, 32),))
    up_weight = noise(key_list[2], (D, FF), D ** -0.5, 0.0625, ((0, 32),))
    skew_params = noise(key_list[3], (MATS, SECTIONS, NB, BLOCK, BLOCK), 0.05, 0.3125, ((2, 32),), jnp.float32)
    section_bits = jax.vmap(lambda own: jax.random.permutation(own, LOG_D))(jax.random.split(key_list[4], SECTIONS)).reshape((SECTIONS, LOG_D)).astype(jnp.int32)
    upstream = noise(part_splits[5], (TOKENS, FF), 0.05, 0.3125, ((1, 32),))
    return {"tokens": tokens, "gate_weight": gate_weight, "up_weight": up_weight, "skew_params": skew_params, "section_bits": section_bits, "upstream": upstream}


def cayley(skew_blocks):
    extent = skew_blocks.shape[-1]
    identity = jnp.eye(extent, dtype=skew_blocks.dtype)
    generator = skew_blocks - jnp.swapaxes(skew_blocks, -1, -2)
    minus_part = identity - generator
    squared = jnp.einsum('...ij,...jk->...ik', minus_part, minus_part, precision=lax.Precision.HIGHEST)
    normal = identity - jnp.einsum('...ij,...jk->...ik', generator, generator, precision=lax.Precision.HIGHEST)
    return jnp.linalg.solve(normal, squared)

def slot_order(section_row, extent):
    positions = jnp.arange(extent, dtype=jnp.int32)
    places = jnp.arange(section_row.shape[0], dtype=jnp.int32)
    digits = jnp.right_shift(positions[:, None], places[None, :]) & 1
    return lax.optimization_barrier(jnp.sum(jnp.left_shift(digits, section_row[None, :]), axis=1)).astype(jnp.int32)

def inverse_order(section_row, extent):
    positions = jnp.arange(extent, dtype=jnp.int32)
    places = jnp.arange(section_row.shape[0], dtype=jnp.int32)
    digits = jnp.right_shift(positions[:, None], section_row[None, :]) & 1
    return lax.optimization_barrier(jnp.sum(jnp.left_shift(digits, places[None, :]), axis=1)).astype(jnp.int32)

def rotate_columns(columns, rotation, orders, inverses):
    kept_inputs = []
    current = columns
    block_count = rotation.shape[1]
    col_count = columns.shape[1]
    for section_at in range(len(orders)):
        permuted = current[orders[section_at]].reshape(block_count, -1, col_count)
        mixed_rows = jnp.einsum('kji,kic->kjc', rotation[section_at].astype(jnp.float32), permuted.astype(jnp.float32)).astype(jnp.bfloat16)
        kept_inputs.append(permuted)
        current = mixed_rows.reshape(current.shape)[inverses[section_at]]
    return (current, kept_inputs)

def unrotate(grad_top, rotation, kept_inputs, orders, inverses):
    block_count = rotation.shape[1]
    col_count = grad_top.shape[1]
    factor_grads = [None] * len(orders)
    current = grad_top
    for section_at in reversed(range(len(orders))):
        permuted = current[orders[section_at]].reshape(block_count, -1, col_count)
        factor_grads[section_at] = jnp.einsum('kjc,kic->kji', permuted.astype(jnp.float32), kept_inputs[section_at].astype(jnp.float32))
        if section_at > 0:
            pulled = jnp.einsum('kji,kjc->kic', rotation[section_at].astype(jnp.float32), permuted.astype(jnp.float32)).astype(jnp.bfloat16)
            current = pulled.reshape(current.shape)[inverses[section_at]]
    return jnp.stack(factor_grads)

def reference(tokens, gate_weight, up_weight, skew_params, section_bits, upstream):
    rotation_f32, pullback = jax.vjp(cayley, skew_params)
    rotation = rotation_f32.astype(jnp.bfloat16)
    model_width = gate_weight.shape[0]
    orders = [slot_order(section_bits[section_at], model_width) for section_at in range(SECTIONS)]
    inverses = [inverse_order(section_bits[section_at], model_width) for section_at in range(SECTIONS)]
    piece_cols = upstream.shape[1] // 16

    def one_piece(factor_sum, piece_index):
        first_col = (piece_index * piece_cols).astype(jnp.int32)
        gate_cols = lax.dynamic_slice_in_dim(gate_weight, first_col, piece_cols, 1)
        up_cols = lax.dynamic_slice_in_dim(up_weight, first_col, piece_cols, 1)
        cotangent = lax.dynamic_slice_in_dim(upstream, first_col, piece_cols, 1).astype(jnp.float32)
        rotated_gate, gate_inputs = rotate_columns(gate_cols, rotation[0], orders, inverses)
        rotated_up, up_inputs = rotate_columns(up_cols, rotation[1], orders, inverses)
        gate_pre = jnp.dot(tokens.astype(jnp.float32), rotated_gate.astype(jnp.float32), preferred_element_type=jnp.float32)
        up_pre = jnp.dot(tokens.astype(jnp.float32), rotated_up.astype(jnp.float32), preferred_element_type=jnp.float32)
        sigmoid_val = jax.nn.sigmoid(gate_pre)
        silu_val = gate_pre * sigmoid_val
        activation = (silu_val * up_pre).astype(jnp.bfloat16)
        gate_grad = (cotangent * up_pre * sigmoid_val * (1.0 + gate_pre * (1.0 - sigmoid_val))).astype(jnp.bfloat16)
        up_grad = (cotangent * silu_val).astype(jnp.bfloat16)
        gate_top = jnp.dot(tokens.T.astype(jnp.float32), gate_grad.astype(jnp.float32), preferred_element_type=jnp.float32).astype(jnp.bfloat16)
        up_top = jnp.dot(tokens.T.astype(jnp.float32), up_grad.astype(jnp.float32), preferred_element_type=jnp.float32).astype(jnp.bfloat16)
        gate_factor = unrotate(gate_top, rotation[0], gate_inputs, orders, inverses)
        up_factor = unrotate(up_top, rotation[1], up_inputs, orders, inverses)
        return (factor_sum + jnp.stack((gate_factor, up_factor)), activation)
    start_sum = jnp.zeros(rotation.shape, jnp.float32)
    factor_sum, act_blocks = lax.scan(one_piece, start_sum, jnp.arange(16, dtype=jnp.int32))
    activation = jnp.transpose(act_blocks, (1, 0, 2)).reshape(tokens.shape[0], upstream.shape[1])
    skew_grad = pullback(factor_sum)[0]
    return (activation, skew_grad)
```

```python
import jax
import jax.numpy as jnp
from jax import lax
from jax.experimental import pallas as pl
from jax.experimental.pallas import tpu as pltpu
from jax.sharding import PartitionSpec as P


def inverse_kernel(skew_ref, out_ref):
    extent = skew_ref.shape[-1]
    shape = skew_ref.shape
    row_at = lax.broadcasted_iota(jnp.int32, shape, 1)
    col_at = lax.broadcasted_iota(jnp.int32, shape, 2)
    skew = skew_ref[...]
    generator = skew - jnp.swapaxes(skew, 1, 2)
    out_ref[...] = jnp.where(row_at == col_at, 1.0, 0.0) + generator
    lane = lax.broadcasted_iota(jnp.int32, (shape[0], 1, extent), 2)

    def step(at, carry):
        work = out_ref[...]
        pivot_row = out_ref[:, pl.ds(at, 1), :]
        at_col = col_at == at
        pivot_col = jnp.sum(jnp.where(at_col, work, 0.0), axis=2, keepdims=True)
        pivot = jnp.sum(jnp.where(lane == at, pivot_row, 0.0), axis=2, keepdims=True)
        scale = 1.0 / pivot
        scaled_row = jnp.where(lane == at, 1.0, pivot_row) * scale
        cleared = jnp.where(at_col, 0.0, work)
        out_ref[...] = cleared - pivot_col * scaled_row
        out_ref[:, pl.ds(at, 1), :] = scaled_row
        return carry

    lax.fori_loop(0, extent, step, 0)


def cayley_inverse(skew_blocks):
    extent = skew_blocks.shape[-1]
    flat = skew_blocks.reshape(-1, extent, extent)
    out = pl.pallas_call(
        inverse_kernel,
        out_shape=jax.ShapeDtypeStruct(flat.shape, jnp.float32),
        in_specs=[pl.BlockSpec(memory_space=pltpu.VMEM)],
        out_specs=pl.BlockSpec(memory_space=pltpu.VMEM),
        cost_estimate=pl.CostEstimate(
            flops=50_000_000, bytes_accessed=2 * 4 * flat.size, transcendentals=0
        ),
        name="cayley_inverse",
    )(flat)
    return out.reshape(skew_blocks.shape)


def slot_order(section_row, extent):
    positions = jnp.arange(extent, dtype=jnp.int32)
    places = jnp.arange(section_row.shape[0], dtype=jnp.int32)
    digits = jnp.right_shift(positions[:, None], places[None, :]) & 1
    return jnp.sum(jnp.left_shift(digits, section_row[None, :]), axis=1)


def inverse_order(section_row, extent):
    positions = jnp.arange(extent, dtype=jnp.int32)
    places = jnp.arange(section_row.shape[0], dtype=jnp.int32)
    digits = jnp.right_shift(positions[:, None], section_row[None, :]) & 1
    return jnp.sum(jnp.left_shift(digits, places[None, :]), axis=1)


def mix(spec, blocks, columns):
    out = jnp.einsum(spec, blocks, columns, preferred_element_type=jnp.float32)
    return out.astype(jnp.bfloat16)


def shards(tokens, gate_weight, up_weight, skew_params, section_bits, upstream):
    mats, _, own_blocks, extent, _ = skew_params.shape
    model_width = tokens.shape[1]
    block_count = model_width // extent
    own_rows = gate_weight.shape[0]
    own_cols = upstream.shape[1]
    devices = gate_weight.shape[1] // own_cols
    half = devices // 2
    half_rows = half * own_rows
    side = lax.axis_index("rows") // half
    groups = [list(range(half)), list(range(half, devices))]
    swap = [(at, (at + half) % devices) for at in range(devices)]

    def move(weight):
        parts = weight.reshape(own_rows, 2, half, own_cols).transpose(2, 0, 1, 3)
        parts = parts.reshape(half, own_rows, 2 * own_cols)
        moved = lax.all_to_all(
            parts, "rows", split_axis=0, concat_axis=0, axis_index_groups=groups, tiled=True
        )
        return moved.reshape(half_rows, 2 * own_cols)

    gate_cols = move(gate_weight)
    up_cols = move(up_weight)

    inverse = cayley_inverse(skew_params)
    own_rotation = (2.0 * inverse - jnp.eye(extent, dtype=jnp.float32)).astype(jnp.bfloat16)
    packed = own_rotation.transpose(2, 3, 0, 1, 4).reshape(own_blocks * extent, -1)
    all_rotation = lax.all_gather(packed, "rows", axis=0, tiled=True)
    all_rotation = all_rotation.reshape(block_count, extent, mats, -1, extent)
    all_tokens = lax.all_gather(tokens, "rows", axis=0, tiled=True)
    token_count = all_tokens.shape[0]
    other_upstream = lax.ppermute(upstream, "rows", swap)

    order_0, order_1 = (slot_order(section_bits[at], model_width) for at in range(2))
    inverse_0, inverse_1 = (inverse_order(section_bits[at], model_width) for at in range(2))

    top_tokens = all_tokens.T[order_1].reshape(block_count, extent, token_count)
    mid = [mix("kji,kjt->kit", all_rotation[:, :, m, 1], top_tokens) for m in range(mats)]
    mid = jnp.concatenate(mid, axis=2).reshape(model_width, -1)
    mid = mid[inverse_1[order_0]].reshape(block_count, extent, mats, token_count)
    low = [mix("kji,kjt->kit", all_rotation[:, :, m, 0], mid[:, :, m]) for m in range(mats)]
    low = jnp.concatenate(low, axis=2).reshape(model_width, -1)
    own_inverse = lax.dynamic_slice(inverse_0, (side * half_rows,), (half_rows,))
    low = low[own_inverse].reshape(half_rows, mats, token_count)

    def project(at, columns):
        part = lax.dot_general(
            low[:, at], columns, (((0,), (0,)), ((), ())), preferred_element_type=jnp.float32
        )
        return part + lax.ppermute(part.astype(jnp.bfloat16), "rows", swap).astype(jnp.float32)

    gate_pre = project(0, gate_cols)
    up_pre = project(1, up_cols)
    sigmoid_val = jax.nn.sigmoid(gate_pre)
    silu_val = gate_pre * sigmoid_val
    activation = (silu_val * up_pre).astype(jnp.bfloat16)
    activation = jnp.where(side == 0, activation[:, :own_cols], activation[:, own_cols:])
    first = jnp.where(side == 0, upstream, other_upstream)
    second = jnp.where(side == 0, other_upstream, upstream)
    cotangent = jnp.concatenate([first, second], axis=1).astype(jnp.float32)
    gate_grad = (cotangent * up_pre * sigmoid_val * (1.0 + gate_pre * (1.0 - sigmoid_val))).astype(
        jnp.bfloat16
    )
    up_grad = (cotangent * silu_val).astype(jnp.bfloat16)

    pulled = [
        lax.dot_general(
            columns, grad, (((1,), (1,)), ((), ())), preferred_element_type=jnp.float32
        ).astype(jnp.bfloat16)
        for columns, grad in ((gate_cols, gate_grad), (up_cols, up_grad))
    ]
    pulled = jnp.concatenate(pulled, axis=1)
    at_row = order_0 - side * half_rows
    held = (at_row >= 0) & (at_row < half_rows)
    pulled = jnp.where(held[:, None], pulled[jnp.clip(at_row, 0, half_rows - 1)], 0)
    pulled = pulled.reshape(block_count, extent, mats, token_count)

    def total(left, right):
        terms = [
            mix("kjt,kit->kji", left[m], right[:, :, m]) for m in range(mats)
        ]
        terms = jnp.concatenate(terms, axis=2).reshape(devices, own_blocks * extent, -1)
        terms = lax.all_to_all(terms, "rows", split_axis=0, concat_axis=0, tiled=True)
        summed = jnp.sum(terms.astype(jnp.float32), axis=0)
        return summed.reshape(own_blocks, extent, mats, extent).transpose(2, 0, 1, 3)

    factor_grad_0 = total([mid[:, :, m] for m in range(mats)], pulled)
    raised = [mix("kji,kit->kjt", all_rotation[:, :, m, 0], pulled[:, :, m]) for m in range(mats)]
    raised = jnp.concatenate(raised, axis=2).reshape(model_width, -1)
    raised = raised[inverse_0[order_1]].reshape(block_count, extent, mats, token_count)
    factor_grad_1 = total([top_tokens] * mats, raised)
    factor_grad = jnp.stack([factor_grad_0, factor_grad_1], axis=1)

    left = jnp.einsum(
        "mskab,mskac->mskbc", inverse, factor_grad, precision=lax.Precision.HIGHEST
    )
    generator_grad = -2.0 * jnp.einsum(
        "mskbc,mskdc->mskbd", left, inverse, precision=lax.Precision.HIGHEST
    )
    skew_grad = generator_grad - jnp.swapaxes(generator_grad, -1, -2)
    return (activation, skew_grad)


def solution(mesh):
    placed = (
        P(("groups", "rows"), None),
        P("rows", None),
        P("rows", None),
        P(None, None, "rows", None, None),
        P(),
        P("groups", "rows"),
    )
    return jax.shard_map(
        shards,
        mesh=mesh,
        in_specs=placed,
        out_specs=(P("groups", "rows"), P("groups", None, "rows", None, None)),
        check_vma=False,
    )
```

```python
import jax
import jax.numpy as jnp
from jax import lax
from jax.experimental import pallas as pl
from jax.experimental.pallas import tpu as pltpu
from jax.sharding import PartitionSpec as P


def inverse_kernel(skew_ref, out_ref):
    extent = skew_ref.shape[-1]
    shape = skew_ref.shape
    row_at = lax.broadcasted_iota(jnp.int32, shape, 1)
    col_at = lax.broadcasted_iota(jnp.int32, shape, 2)
    skew = skew_ref[...]
    generator = skew - jnp.swapaxes(skew, 1, 2)
    out_ref[...] = jnp.where(row_at == col_at, 1.0, 0.0) + generator
    lane = lax.broadcasted_iota(jnp.int32, (shape[0], 1, extent), 2)

    def step(at, carry):
        work = out_ref[...]
        pivot_row = out_ref[:, pl.ds(at, 1), :]
        at_col = col_at == at
        pivot_col = jnp.sum(jnp.where(at_col, work, 0.0), axis=2, keepdims=True)
        pivot = jnp.sum(jnp.where(lane == at, pivot_row, 0.0), axis=2, keepdims=True)
        scale = 1.0 / pivot
        scaled_row = jnp.where(lane == at, 1.0, pivot_row) * scale
        cleared = jnp.where(at_col, 0.0, work)
        out_ref[...] = cleared - pivot_col * scaled_row
        out_ref[:, pl.ds(at, 1), :] = scaled_row
        return carry

    lax.fori_loop(0, extent, step, 0)


def cayley_inverse(skew_blocks):
    extent = skew_blocks.shape[-1]
    flat = skew_blocks.reshape(-1, extent, extent)
    out = pl.pallas_call(
        inverse_kernel,
        out_shape=jax.ShapeDtypeStruct(flat.shape, jnp.float32),
        in_specs=[pl.BlockSpec(memory_space=pltpu.VMEM)],
        out_specs=pl.BlockSpec(memory_space=pltpu.VMEM),
        cost_estimate=pl.CostEstimate(
            flops=50_000_000, bytes_accessed=2 * 4 * flat.size, transcendentals=0
        ),
        name="cayley_inverse",
    )(flat)
    return out.reshape(skew_blocks.shape)


def estimate(flops, *arrays):
    moved = sum(array.size * array.dtype.itemsize for array in arrays)
    return pl.CostEstimate(flops=flops, bytes_accessed=moved, transcendentals=0)


def pack(weight, half, cols):
    rows, width = weight.shape
    step = min(rows, 32)

    def body(in_ref, out_ref):
        for at in range(half):
            left = in_ref[:, at * cols : (at + 1) * cols]
            right = in_ref[:, (half + at) * cols : (half + at + 1) * cols]
            out_ref[at] = jnp.concatenate([left, right], axis=1)

    out = jax.ShapeDtypeStruct((half, rows, 2 * cols), weight.dtype)
    return pl.pallas_call(
        body,
        out_shape=out,
        grid=(rows // step,),
        in_specs=[pl.BlockSpec((step, width), lambda at: (at, 0))],
        out_specs=pl.BlockSpec((half, step, 2 * cols), lambda at: (0, at, 0)),
        cost_estimate=estimate(0, weight, out),
        name="pack",
    )(weight)


def blocked(body, name, extent, inputs, out_widths):
    rows = inputs[0].shape[0]
    step = min(8 * extent, rows)
    outs = tuple(jax.ShapeDtypeStruct((rows, width), jnp.bfloat16) for width in out_widths)
    return pl.pallas_call(
        body,
        out_shape=outs,
        grid=(rows // step,),
        in_specs=[pl.BlockSpec((step, array.shape[1]), lambda at: (at, 0)) for array in inputs],
        out_specs=tuple(pl.BlockSpec((step, width), lambda at: (at, 0)) for width in out_widths),
        cost_estimate=estimate(4 * rows * extent * out_widths[-1], *inputs, *outs),
        name=name,
    )(*inputs)


def dot(left, right, left_dim, right_dim):
    contract = (((left_dim,), (right_dim,)), ((), ()))
    return lax.dot_general(left, right, contract, preferred_element_type=jnp.float32)


def mix(rotation, columns, section, extent, mats, count):
    shared = columns.shape[1] == count
    pair = mats * extent

    def body(rotation_ref, in_ref, out_ref):
        for at in range(in_ref.shape[0] // extent):
            rows = slice(at * extent, (at + 1) * extent)
            blocks = rotation_ref[rows, section * pair : (section + 1) * pair]
            if shared:
                mixed = dot(blocks, in_ref[rows, :], 0, 0).astype(jnp.bfloat16)
            for m in range(mats):
                lanes = slice(m * count, (m + 1) * count)
                if shared:
                    out_ref[rows, lanes] = mixed[m * extent : (m + 1) * extent]
                else:
                    own = blocks[:, m * extent : (m + 1) * extent]
                    out_ref[rows, lanes] = dot(own, in_ref[rows, lanes], 0, 0).astype(jnp.bfloat16)

    return blocked(body, "mix", extent, (rotation, columns), (mats * count,))[0]


def raise_terms(rotation, left, right, extent, mats, count):
    def body(rotation_ref, left_ref, right_ref, terms_ref, out_ref):
        for at in range(left_ref.shape[0] // extent):
            rows = slice(at * extent, (at + 1) * extent)
            terms = []
            for m in range(mats):
                lanes = slice(m * count, (m + 1) * count)
                pulled = right_ref[rows, lanes]
                terms.append(dot(left_ref[rows, lanes], pulled, 1, 1))
                own = rotation_ref[rows, m * extent : (m + 1) * extent]
                out_ref[rows, lanes] = dot(own, pulled, 1, 0).astype(jnp.bfloat16)
            terms_ref[rows, :] = jnp.concatenate(terms, axis=1).astype(jnp.bfloat16)

    return blocked(
        body, "raise_terms", extent, (rotation, left, right), (mats * extent, mats * count)
    )


def top_terms(left, right, extent, mats, count):
    def body(left_ref, right_ref, terms_ref):
        for at in range(left_ref.shape[0] // extent):
            rows = slice(at * extent, (at + 1) * extent)
            terms = [
                dot(left_ref[rows, :], right_ref[rows, m * count : (m + 1) * count], 1, 1)
                for m in range(mats)
            ]
            terms_ref[rows, :] = jnp.concatenate(terms, axis=1).astype(jnp.bfloat16)

    return blocked(body, "top_terms", extent, (left, right), (mats * extent,))[0]


def pull(gate_cols, up_cols, gate_grad, up_grad):
    rows, width = gate_cols.shape
    count = gate_grad.shape[0]
    step = min(512, rows)
    last = rows // step - 1

    def body(gate_ref, up_ref, gate_grad_ref, up_grad_ref, out_ref):
        @pl.when(pl.program_id(0) <= last)
        def _():
            out_ref[:, :count] = dot(gate_ref[...], gate_grad_ref[...], 1, 1).astype(jnp.bfloat16)
            out_ref[:, count:] = dot(up_ref[...], up_grad_ref[...], 1, 1).astype(jnp.bfloat16)

        @pl.when(pl.program_id(0) > last)
        def _():
            out_ref[...] = jnp.zeros_like(out_ref)

    out = jax.ShapeDtypeStruct((rows + step, 2 * count), jnp.bfloat16)
    weights = pl.BlockSpec((step, width), lambda at: (jnp.minimum(at, last), 0))
    grads = pl.BlockSpec((count, width), lambda at: (0, 0))
    return pl.pallas_call(
        body,
        out_shape=out,
        grid=(last + 2,),
        in_specs=[weights, weights, grads, grads],
        out_specs=pl.BlockSpec((step, 2 * count), lambda at: (at, 0)),
        cost_estimate=estimate(4 * rows * width * count, gate_cols, up_cols, out),
        name="pull",
    )(gate_cols, up_cols, gate_grad, up_grad)


def slot_order(section_row, positions):
    places = jnp.arange(section_row.shape[0], dtype=jnp.int32)
    digits = jnp.right_shift(positions[:, None], places[None, :]) & 1
    return jnp.sum(jnp.left_shift(digits, section_row[None, :]), axis=1)


def places_of(bits, section_row):
    places = jnp.arange(section_row.shape[0], dtype=jnp.int32)
    found = bits[:, None] == section_row[None, :]
    return jnp.sum(jnp.where(found, places[None, :], 0), axis=1)


def take(array, index):
    return array.at[index].get(mode="promise_in_bounds")


def shards(tokens, gate_weight, up_weight, skew_params, section_bits, upstream):
    mats, _, own_blocks, extent, _ = skew_params.shape
    model_width = tokens.shape[1]
    own_rows = gate_weight.shape[0]
    own_cols = upstream.shape[1]
    devices = gate_weight.shape[1] // own_cols
    half = devices // 2
    half_rows = half * own_rows
    side = lax.axis_index("rows") // half
    groups = [list(range(half)), list(range(half, devices))]
    swap = [(at, (at + half) % devices) for at in range(devices)]

    def move(parts):
        moved = lax.all_to_all(
            parts, "rows", split_axis=0, concat_axis=0, axis_index_groups=groups, tiled=True
        )
        return moved.reshape(half_rows, 2 * own_cols)

    all_tokens = lax.all_gather(tokens, "rows", axis=0, tiled=True)
    token_count = all_tokens.shape[0]
    gate_parts, skew_params = lax.optimization_barrier(
        (pack(gate_weight, half, own_cols), skew_params)
    )
    gate_cols = move(gate_parts)
    up_cols = move(pack(up_weight, half, own_cols))

    inverse = cayley_inverse(skew_params)
    own_rotation = (2.0 * inverse - jnp.eye(extent, dtype=jnp.float32)).astype(jnp.bfloat16)
    packed = own_rotation.transpose(2, 3, 1, 0, 4).reshape(own_blocks * extent, -1)
    packed, all_tokens = lax.optimization_barrier((packed, all_tokens))
    rotation = lax.all_gather(packed, "rows", axis=0, tiled=True)
    other_upstream = lax.ppermute(upstream, "rows", swap)

    positions = jnp.arange(model_width, dtype=jnp.int32)
    bits_0, bits_1 = section_bits[0], section_bits[1]
    order_0 = slot_order(bits_0, positions)
    order_1 = slot_order(bits_1, positions)
    one_to_zero = slot_order(places_of(bits_0, bits_1), positions)
    zero_to_one = slot_order(places_of(bits_1, bits_0), positions)
    natural = jnp.arange(bits_0.shape[0], dtype=jnp.int32)
    own_positions = side * half_rows + jnp.arange(half_rows, dtype=jnp.int32)
    own_inverse = slot_order(places_of(natural, bits_0), own_positions)

    sizes = (extent, mats, token_count)
    top_tokens = take(all_tokens.T, order_1)
    mid = take(mix(rotation, top_tokens, 1, *sizes), one_to_zero)
    low = take(mix(rotation, mid, 0, *sizes), own_inverse)

    def project(at, columns):
        part = dot(low[:, at * token_count : (at + 1) * token_count], columns, 0, 0)
        return part + lax.ppermute(part.astype(jnp.bfloat16), "rows", swap).astype(jnp.float32)

    gate_pre = project(0, gate_cols)
    up_pre = project(1, up_cols)
    sigmoid_val = jax.nn.sigmoid(gate_pre)
    silu_val = gate_pre * sigmoid_val
    activation = (silu_val * up_pre).astype(jnp.bfloat16)
    activation = jnp.where(side == 0, activation[:, :own_cols], activation[:, own_cols:])
    first = jnp.where(side == 0, upstream, other_upstream)
    second = jnp.where(side == 0, other_upstream, upstream)
    cotangent = jnp.concatenate([first, second], axis=1).astype(jnp.float32)
    gate_grad = (cotangent * up_pre * sigmoid_val * (1.0 + gate_pre * (1.0 - sigmoid_val))).astype(
        jnp.bfloat16
    )
    up_grad = (cotangent * silu_val).astype(jnp.bfloat16)

    at_row = order_0 - side * half_rows
    held = (at_row >= 0) & (at_row < half_rows)
    pulled = take(pull(gate_cols, up_cols, gate_grad, up_grad), jnp.where(held, at_row, half_rows))

    def total(terms):
        terms = terms.reshape(devices, own_blocks * extent, -1)
        terms = lax.all_to_all(terms, "rows", split_axis=0, concat_axis=0, tiled=True)
        summed = jnp.sum(terms.astype(jnp.float32), axis=0)
        return summed.reshape(own_blocks, extent, mats, extent).transpose(2, 0, 1, 3)

    terms_0, raised = raise_terms(rotation, mid, pulled, *sizes)
    factor_grad_0 = total(terms_0)
    raised = take(raised, zero_to_one)
    factor_grad_1 = total(top_terms(top_tokens, raised, *sizes))
    factor_grad = jnp.stack([factor_grad_0, factor_grad_1], axis=1)

    left = jnp.einsum(
        "mskab,mskac->mskbc", inverse, factor_grad, precision=lax.Precision.HIGHEST
    )
    generator_grad = -2.0 * jnp.einsum(
        "mskbc,mskdc->mskbd", left, inverse, precision=lax.Precision.HIGHEST
    )
    skew_grad = generator_grad - jnp.swapaxes(generator_grad, -1, -2)
    return (activation, skew_grad)


def solution(mesh):
    placed = (
        P(("groups", "rows"), None),
        P("rows", None),
        P("rows", None),
        P(None, None, "rows", None, None),
        P(),
        P("groups", "rows"),
    )
    return jax.shard_map(
        shards,
        mesh=mesh,
        in_specs=placed,
        out_specs=(P("groups", "rows"), P("groups", None, "rows", None, None)),
        check_vma=False,
    )
```

```python
import jax
import jax.numpy as jnp
from jax import lax
from jax.experimental import pallas as pl
from jax.experimental.pallas import tpu as pltpu
from jax.sharding import PartitionSpec as P


def inverse_kernel(skew_ref, out_ref):
    extent = skew_ref.shape[-1]
    shape = skew_ref.shape
    row_at = lax.broadcasted_iota(jnp.int32, shape, 1)
    col_at = lax.broadcasted_iota(jnp.int32, shape, 2)
    skew = skew_ref[...]
    generator = skew - jnp.swapaxes(skew, 1, 2)
    out_ref[...] = jnp.where(row_at == col_at, 1.0, 0.0) + generator
    lane = lax.broadcasted_iota(jnp.int32, (shape[0], 1, extent), 2)

    def step(at, carry):
        work = out_ref[...]
        pivot_row = out_ref[:, pl.ds(at, 1), :]
        at_col = col_at == at
        pivot_col = jnp.sum(jnp.where(at_col, work, 0.0), axis=2, keepdims=True)
        pivot = jnp.sum(jnp.where(lane == at, pivot_row, 0.0), axis=2, keepdims=True)
        scale = 1.0 / pivot
        scaled_row = jnp.where(lane == at, 1.0, pivot_row) * scale
        cleared = jnp.where(at_col, 0.0, work)
        out_ref[...] = cleared - pivot_col * scaled_row
        out_ref[:, pl.ds(at, 1), :] = scaled_row
        return carry

    lax.fori_loop(0, extent, step, 0)


def cayley_inverse(skew_blocks):
    extent = skew_blocks.shape[-1]
    flat = skew_blocks.reshape(-1, extent, extent)
    out = pl.pallas_call(
        inverse_kernel,
        out_shape=jax.ShapeDtypeStruct(flat.shape, jnp.float32),
        in_specs=[pl.BlockSpec(memory_space=pltpu.VMEM)],
        out_specs=pl.BlockSpec(memory_space=pltpu.VMEM),
        cost_estimate=pl.CostEstimate(
            flops=50_000_000, bytes_accessed=2 * 4 * flat.size, transcendentals=0
        ),
        name="cayley_inverse",
    )(flat)
    return out.reshape(skew_blocks.shape)


def estimate(flops, *arrays):
    moved = sum(array.size * array.dtype.itemsize for array in arrays)
    return pl.CostEstimate(flops=flops, bytes_accessed=moved, transcendentals=0)


def pack(weight, half, cols):
    rows, width = weight.shape
    step = min(rows, 32)

    def body(in_ref, out_ref):
        for at in range(half):
            left = in_ref[:, at * cols : (at + 1) * cols]
            right = in_ref[:, (half + at) * cols : (half + at + 1) * cols]
            out_ref[at] = jnp.concatenate([left, right], axis=1)

    out = jax.ShapeDtypeStruct((half, rows, 2 * cols), weight.dtype)
    return pl.pallas_call(
        body,
        out_shape=out,
        grid=(rows // step,),
        in_specs=[pl.BlockSpec((step, width), lambda at: (at, 0))],
        out_specs=pl.BlockSpec((half, step, 2 * cols), lambda at: (0, at, 0)),
        cost_estimate=estimate(0, weight, out),
        name="pack",
    )(weight)


def blocked(body, name, extent, inputs, out_widths):
    rows = inputs[0].shape[0]
    step = min(8 * extent, rows)
    outs = tuple(jax.ShapeDtypeStruct((rows, width), jnp.bfloat16) for width in out_widths)
    return pl.pallas_call(
        body,
        out_shape=outs,
        grid=(rows // step,),
        in_specs=[pl.BlockSpec((step, array.shape[1]), lambda at: (at, 0)) for array in inputs],
        out_specs=tuple(pl.BlockSpec((step, width), lambda at: (at, 0)) for width in out_widths),
        cost_estimate=estimate(4 * rows * extent * out_widths[-1], *inputs, *outs),
        name=name,
    )(*inputs)


def dot(left, right, left_dim, right_dim):
    contract = (((left_dim,), (right_dim,)), ((), ()))
    return lax.dot_general(left, right, contract, preferred_element_type=jnp.float32)


def mix(rotation, columns, section, extent, mats, count):
    shared = columns.shape[1] == count
    pair = mats * extent

    def body(rotation_ref, in_ref, out_ref):
        for at in range(in_ref.shape[0] // extent):
            rows = slice(at * extent, (at + 1) * extent)
            blocks = rotation_ref[rows, section * pair : (section + 1) * pair]
            if shared:
                mixed = dot(blocks, in_ref[rows, :], 0, 0).astype(jnp.bfloat16)
            for m in range(mats):
                lanes = slice(m * count, (m + 1) * count)
                if shared:
                    out_ref[rows, lanes] = mixed[m * extent : (m + 1) * extent]
                else:
                    own = blocks[:, m * extent : (m + 1) * extent]
                    out_ref[rows, lanes] = dot(own, in_ref[rows, lanes], 0, 0).astype(jnp.bfloat16)

    return blocked(body, "mix", extent, (rotation, columns), (mats * count,))[0]


def raise_terms(rotation, left, right, extent, mats, count):
    def body(rotation_ref, left_ref, right_ref, terms_ref, out_ref):
        for at in range(left_ref.shape[0] // extent):
            rows = slice(at * extent, (at + 1) * extent)
            terms = []
            for m in range(mats):
                lanes = slice(m * count, (m + 1) * count)
                pulled = right_ref[rows, lanes]
                terms.append(dot(left_ref[rows, lanes], pulled, 1, 1))
                own = rotation_ref[rows, m * extent : (m + 1) * extent]
                out_ref[rows, lanes] = dot(own, pulled, 1, 0).astype(jnp.bfloat16)
            terms_ref[rows, :] = jnp.concatenate(terms, axis=1).astype(jnp.bfloat16)

    return blocked(
        body, "raise_terms", extent, (rotation, left, right), (mats * extent, mats * count)
    )


def top_terms(left, right, extent, mats, count):
    def body(left_ref, right_ref, terms_ref):
        for at in range(left_ref.shape[0] // extent):
            rows = slice(at * extent, (at + 1) * extent)
            terms = [
                dot(left_ref[rows, :], right_ref[rows, m * count : (m + 1) * count], 1, 1)
                for m in range(mats)
            ]
            terms_ref[rows, :] = jnp.concatenate(terms, axis=1).astype(jnp.bfloat16)

    return blocked(body, "top_terms", extent, (left, right), (mats * extent,))[0]


def pull(gate_cols, up_cols, gate_grad, up_grad):
    rows, width = gate_cols.shape
    count = gate_grad.shape[0]
    step = min(512, rows)
    last = rows // step - 1

    def body(gate_ref, up_ref, gate_grad_ref, up_grad_ref, out_ref):
        @pl.when(pl.program_id(0) <= last)
        def _():
            out_ref[:, :count] = dot(gate_ref[...], gate_grad_ref[...], 1, 1).astype(jnp.bfloat16)
            out_ref[:, count:] = dot(up_ref[...], up_grad_ref[...], 1, 1).astype(jnp.bfloat16)

        @pl.when(pl.program_id(0) > last)
        def _():
            out_ref[...] = jnp.zeros_like(out_ref)

    out = jax.ShapeDtypeStruct((rows + step, 2 * count), jnp.bfloat16)
    weights = pl.BlockSpec((step, width), lambda at: (jnp.minimum(at, last), 0))
    grads = pl.BlockSpec((count, width), lambda at: (0, 0))
    return pl.pallas_call(
        body,
        out_shape=out,
        grid=(last + 2,),
        in_specs=[weights, weights, grads, grads],
        out_specs=pl.BlockSpec((step, 2 * count), lambda at: (at, 0)),
        cost_estimate=estimate(4 * rows * width * count, gate_cols, up_cols, out),
        name="pull",
    )(gate_cols, up_cols, gate_grad, up_grad)


def slot_order(section_row, positions):
    places = jnp.arange(section_row.shape[0], dtype=jnp.int32)
    digits = jnp.right_shift(positions[:, None], places[None, :]) & 1
    return jnp.sum(jnp.left_shift(digits, section_row[None, :]), axis=1)


def places_of(bits, section_row):
    places = jnp.arange(section_row.shape[0], dtype=jnp.int32)
    found = bits[:, None] == section_row[None, :]
    return jnp.sum(jnp.where(found, places[None, :], 0), axis=1)


def take(array, index):
    return array.at[index].get(mode="promise_in_bounds")


def shards(tokens, gate_weight, up_weight, skew_params, section_bits, upstream):
    mats, _, own_blocks, extent, _ = skew_params.shape
    model_width = tokens.shape[1]
    own_rows = gate_weight.shape[0]
    own_cols = upstream.shape[1]
    devices = gate_weight.shape[1] // own_cols
    half = devices // 2
    half_rows = half * own_rows
    side = lax.axis_index("rows") // half
    groups = [list(range(half)), list(range(half, devices))]
    swap = [(at, (at + half) % devices) for at in range(devices)]

    def move(parts):
        moved = lax.all_to_all(
            parts, "rows", split_axis=0, concat_axis=0, axis_index_groups=groups, tiled=True
        )
        return moved.reshape(half_rows, 2 * own_cols)

    all_tokens = lax.all_gather(tokens, "rows", axis=0, tiled=True)
    token_count = all_tokens.shape[0]
    inverse = cayley_inverse(skew_params)
    own_rotation = (2.0 * inverse - jnp.eye(extent, dtype=jnp.float32)).astype(jnp.bfloat16)
    packed = own_rotation.transpose(2, 3, 1, 0, 4).reshape(own_blocks * extent, -1)
    packed, gate_parts, all_tokens = lax.optimization_barrier(
        (packed, pack(gate_weight, half, own_cols), all_tokens)
    )
    gate_cols = move(gate_parts)
    rotation = lax.all_gather(packed, "rows", axis=0, tiled=True)
    other_upstream = lax.ppermute(upstream, "rows", swap)

    positions = jnp.arange(model_width, dtype=jnp.int32)
    bits_0, bits_1 = section_bits[0], section_bits[1]
    order_0 = slot_order(bits_0, positions)
    order_1 = slot_order(bits_1, positions)
    one_to_zero = slot_order(places_of(bits_0, bits_1), positions)
    zero_to_one = slot_order(places_of(bits_1, bits_0), positions)
    natural = jnp.arange(bits_0.shape[0], dtype=jnp.int32)
    own_positions = side * half_rows + jnp.arange(half_rows, dtype=jnp.int32)
    own_inverse = slot_order(places_of(natural, bits_0), own_positions)

    sizes = (extent, mats, token_count)
    top_tokens, up_parts, rotation = lax.optimization_barrier(
        (take(all_tokens.T, order_1), pack(up_weight, half, own_cols), rotation)
    )
    up_cols = move(up_parts)
    mid = take(mix(rotation, top_tokens, 1, *sizes), one_to_zero)
    low = take(mix(rotation, mid, 0, *sizes), own_inverse)

    def project(at, columns):
        part = dot(low[:, at * token_count : (at + 1) * token_count], columns, 0, 0)
        return part + lax.ppermute(part.astype(jnp.bfloat16), "rows", swap).astype(jnp.float32)

    gate_pre = project(0, gate_cols)
    up_pre = project(1, up_cols)
    sigmoid_val = jax.nn.sigmoid(gate_pre)
    silu_val = gate_pre * sigmoid_val
    activation = (silu_val * up_pre).astype(jnp.bfloat16)
    activation = jnp.where(side == 0, activation[:, :own_cols], activation[:, own_cols:])
    first = jnp.where(side == 0, upstream, other_upstream)
    second = jnp.where(side == 0, other_upstream, upstream)
    cotangent = jnp.concatenate([first, second], axis=1).astype(jnp.float32)
    gate_grad = (cotangent * up_pre * sigmoid_val * (1.0 + gate_pre * (1.0 - sigmoid_val))).astype(
        jnp.bfloat16
    )
    up_grad = (cotangent * silu_val).astype(jnp.bfloat16)

    at_row = order_0 - side * half_rows
    held = (at_row >= 0) & (at_row < half_rows)
    pulled = take(pull(gate_cols, up_cols, gate_grad, up_grad), jnp.where(held, at_row, half_rows))

    def send(terms):
        terms = terms.reshape(devices, own_blocks * extent, -1)
        return lax.all_to_all(terms, "rows", split_axis=0, concat_axis=0, tiled=True)

    def summed_of(terms):
        summed = jnp.sum(terms.astype(jnp.float32), axis=0)
        return summed.reshape(own_blocks, extent, mats, extent).transpose(2, 0, 1, 3)

    terms_0, raised = raise_terms(rotation, mid, pulled, *sizes)
    sent_0, raised = lax.optimization_barrier((send(terms_0), take(raised, zero_to_one)))
    sent_1 = send(top_terms(top_tokens, raised, *sizes))
    factor_grad = jnp.stack([summed_of(sent_0), summed_of(sent_1)], axis=1)

    left = jnp.einsum(
        "mskab,mskac->mskbc", inverse, factor_grad, precision=lax.Precision.HIGHEST
    )
    generator_grad = -2.0 * jnp.einsum(
        "mskbc,mskdc->mskbd", left, inverse, precision=lax.Precision.HIGHEST
    )
    skew_grad = generator_grad - jnp.swapaxes(generator_grad, -1, -2)
    return (activation, skew_grad)


def solution(mesh):
    placed = (
        P(("groups", "rows"), None),
        P("rows", None),
        P("rows", None),
        P(None, None, "rows", None, None),
        P(),
        P("groups", "rows"),
    )
    return jax.shard_map(
        shards,
        mesh=mesh,
        in_specs=placed,
        out_specs=(P("groups", "rows"), P("groups", None, "rows", None, None)),
        check_vma=False,
    )
```
